512 devices in a mesh: frames: 64 (over z, y), strips: 8 (over x, core).
Axes of the slice: x: 4, y: 4, z: 16, core: 2. Of those that a mesh axis runs over, the one named last changes fastest.
Arguments:
- raw_frames: bfloat16 [4096, 512, 512], P('frames', 'strips'), may hold values from -24 to 24
- dark_frame: float32 [512, 512], P('strips'), may hold values from -6 to 6
- dead_mask: int32 [512, 512], P('strips'), may hold values 0 or 1
- frame_group: int32 [4096], P('frames'), may hold values from 0 to 7
- prior_sigma: float32 [128], replicated, may hold values from 0.2 to 0.5
- start_rotation: float32 [128, 128], replicated, as said below
- basis: bfloat16 [262144, 128], P(('strips', 'frames')), may hold values from -0.01171875 to 0.01171875
Outputs:
- new_basis: bfloat16 [262144, 128], P(('strips', 'frames'))
- new_coeffs: float32 [4096, 128], P('frames')
- new_sigma: float32 [128], replicated
The draws below stay inside these ranges and needn't reach their ends.
Inputs may be any that keep to these rules, and one draw needn't show every extreme that they name: start_rotation is nonsingular.
All inputs are finite; a program needn't handle non-finite values. No bound on the sum of `dead_mask` on one device may be relied on, other than what follows from the above.
Results may differ from the reference program's by a relative error of at most 0.0071.
Values may be sent and summed in bfloat16 or wider, within the bound.
A program may use at most 64 MiB of HBM per device.

```python
import math
import jax
import jax.numpy as jnp
from jax import lax

H = 512
W = 512
K = 128
F_DEV = 64
GROUPS = 8
ITERS = 4
FRAMES = 4096


def draw_frame_group(key, part):
    frame_index = jnp.arange(FRAMES, dtype=jnp.int32)
    centre = frame_index * GROUPS // FRAMES
    jitter = jax.random.randint(key, (FRAMES,), -2, 3, dtype=jnp.int32)
    group = jnp.clip(centre + jitter, 0, GROUPS - 1)
    group = group.at[0].set(0)
    group = group.at[FRAMES - 1].set(GROUPS - 1)
    return group.astype(jnp.int32)


def draw_start_rotation(key, part):
    position = jnp.arange(K)
    identity = (position[:, None] == position[None, :]).astype(jnp.float32)
    noise = jax.random.normal(key, (K, K), jnp.float32)
    return (identity + 0.25 / math.sqrt(K) * noise).astype(jnp.float32)


def set_ends(entries, rng, least, top_value):
    spot = [jax.random.randint(jax.random.fold_in(rng, axis), (), 0, length) for axis, length in enumerate(entries.shape)]
    longest = entries.shape.index(max(entries.shape))
    beside = spot[:longest] + [(spot[longest] + 1) % entries.shape[longest]] + spot[longest + 1:]
    return entries.at[tuple(spot)].set(least).at[tuple(beside)].set(top_value)


def steps_of(key, shape, cuts, smallest, largest):
    level, own = 1.0, jax.random.fold_in(key, 6)
    for dim, parts in cuts:
        steps = jnp.exp(jax.random.uniform(jax.random.fold_in(own, dim), (parts,), jnp.float32, smallest / len(cuts), largest / len(cuts)))
        level = level * jnp.repeat(steps, shape[dim] // parts).reshape([-1 if axis == dim else 1 for axis in range(len(shape))])
    return level


def normal_values(rng, shape, spread, most, split=(), kind=jnp.bfloat16):
    gain = steps_of(rng, shape, split, -0.22, 0.18) if split else 1.0
    drawn = jax.random.normal(rng, shape, jnp.float32) * spread * gain
    return jnp.minimum(jnp.maximum(drawn, -most), most).astype(kind)


def setup_inputs(seed: int = 0) -> dict:
    keys = jax.random.split(jax.random.key(seed), 8)
    return {
        "raw_frames": normal_values(keys[0], (FRAMES, H, W), 4.0, 24.0, ((0, 64), (1, 8))),
        "dark_frame": normal_values(keys[1], (H, W), 1.0, 6.0, ((0, 8),), jnp.float32),
        "dead_mask": set_ends((jax.random.randint(keys[2], (H, W), 0, 20) < 1).astype(jnp.int32), jax.random.fold_in(keys[2], 1), 0, 1),
        "frame_group": draw_frame_group(jax.random.fold_in(keys[7], 71), 0),
        "prior_sigma": jnp.clip(jnp.exp(jax.random.uniform(keys[4], (K,), jnp.float32, math.log(0.2), math.log(0.5))), 0.2, 0.5),
        "start_rotation": draw_start_rotation(jax.random.fold_in(keys[7], 71), 0),
        "basis": normal_values(keys[6], (H * W, K), (H * W) ** -0.5, 0.01171875, ((0, 512),)),
    }


BLUR_TAPS = (1.0 / 64, 6.0 / 64, 15.0 / 64, 20.0 / 64, 15.0 / 64, 6.0 / 64, 1.0 / 64)
DECAY_RATE = 0.7

def weighted_frames(raw, group, dark_frame, dead_mask):
    corrected = ((raw.astype(jnp.float32) - dark_frame) * (1 - dead_mask).astype(jnp.float32)).astype(jnp.bfloat16)
    corrected = lax.optimization_barrier(corrected).astype(jnp.float32)
    padded = jnp.pad(corrected, ((0, 0), (0, 0), (3, 3)))
    column_blur = BLUR_TAPS[0] * padded[:, :, 0:W]
    for offset in range(1, 7):
        column_blur = column_blur + BLUR_TAPS[offset] * padded[:, :, offset:offset + W]
    padded = jnp.pad(column_blur, ((0, 0), (3, 3), (0, 0)))
    row_blur = BLUR_TAPS[0] * padded[:, 0:H, :]
    for offset in range(1, 7):
        row_blur = row_blur + BLUR_TAPS[offset] * padded[:, offset:offset + H, :]
    frame_weight = jnp.power(jnp.float32(DECAY_RATE), (GROUPS - 1 - group).astype(jnp.float32))
    weighted = (frame_weight[:, None, None] * row_blur).astype(jnp.bfloat16)
    return weighted.reshape(raw.shape[0], H * W)

def orthonormalize(product):
    normal = jnp.dot(product.T, product, precision=lax.Precision.HIGHEST)
    factor = jnp.linalg.cholesky(normal)
    return lax.linalg.triangular_solve(factor, product, left_side=False, lower=True, transpose_a=True)

def reference(raw_frames, dark_frame, dead_mask, frame_group, prior_sigma, start_rotation, basis):
    raw_blocks = raw_frames.reshape(FRAMES // F_DEV, F_DEV, H, W)
    group_blocks = frame_group.reshape(FRAMES // F_DEV, F_DEV)

    def project(item):
        raw, group = item
        weighted = weighted_frames(raw, group, dark_frame, dead_mask)
        return jnp.dot(weighted.astype(jnp.float32), basis.astype(jnp.float32), preferred_element_type=jnp.float32)
    coeffs = lax.map(project, (raw_blocks, group_blocks)).reshape(FRAMES, K)
    gram = jnp.diag(prior_sigma * prior_sigma) + jnp.dot(coeffs.T, coeffs, precision=lax.Precision.HIGHEST) / FRAMES
    rotation = start_rotation
    for step in range(ITERS):
        rotation = orthonormalize(jnp.dot(gram, rotation, precision=lax.Precision.HIGHEST))
    new_coeffs = jnp.dot(coeffs, rotation, precision=lax.Precision.HIGHEST)
    new_basis = jnp.dot(basis.astype(jnp.float32), rotation, precision=lax.Precision.HIGHEST).astype(jnp.bfloat16)
    curved = jnp.dot(gram, rotation, precision=lax.Precision.HIGHEST)
    new_sigma = jnp.sqrt(lax.optimization_barrier(jnp.sum(rotation * curved, axis=0)))
    return (new_basis, new_coeffs, new_sigma)
```

```python
import functools

import jax
import jax.numpy as jnp
from jax import lax
from jax.experimental import pallas as pl
from jax.experimental.pallas import tpu as pltpu
from jax.sharding import PartitionSpec as P

GROUPS = 8
ITERS = 4
K = 128
Y = 4

BLUR_TAPS = (1.0 / 64, 6.0 / 64, 15.0 / 64, 20.0 / 64, 15.0 / 64, 6.0 / 64, 1.0 / 64)
DECAY_RATE = 0.7
MESH = pl.DeviceIdType.MESH
HIGHEST = lax.Precision.HIGHEST


def extended(shard, sides, width):
    for axis, dim in sides:
        size, length = (lax.axis_size(axis), shard.shape[dim])
        up = [(i, (i + 1) % size) for i in range(size - 1)]
        down = [(j, i) for i, j in up]
        last = lax.slice_in_dim(shard, length - width, length, axis=dim)
        first = lax.slice_in_dim(shard, 0, width, axis=dim)
        before = lax.ppermute(last, axis, up)
        after = lax.ppermute(first, axis, down)
        shard = jnp.concatenate([before, shard, after], axis=dim)
    return shard


def reduce_kernel(Z, S, part_ref, coeffs_ref, gram_ref,
                  parts, local, ybuf, zbuf, full,
                  s1, r1, s2, r2, s3, r3, s4, r4):
    f, s = lax.axis_index("frames"), lax.axis_index("strips")
    z, y = f // Y, f % Y
    NB = 2 * S
    rows = K // NB
    strip_peers = [(f, (s + d) % S) for d in range(1, S)]
    y_peers = [(z * Y + (y + d) % Y, s) for d in range(1, Y)]
    z_peers = [(((z + d) % Z) * Y + y, s) for d in range(1, Z)]
    f_cross = z * Y + (y + 2) % Y
    cross_peers = [(f_cross, (s + d) % S) for d in range(1, S)]
    barrier = pltpu.get_barrier_semaphore()
    everyone = strip_peers + y_peers + z_peers + cross_peers
    for peer in everyone:
        pl.semaphore_signal(barrier, inc=1, device_id=peer, device_id_type=MESH)
    pl.semaphore_wait(barrier, len(everyone))

    def send(src, dst, ssem, rsem, peer):
        copy = pltpu.make_async_remote_copy(
            src_ref=src, dst_ref=dst, send_sem=ssem, recv_sem=rsem,
            device_id=peer, device_id_type=MESH)
        copy.start()
        return copy

    def arrived(ref, sem):
        pltpu.make_async_copy(ref, ref, sem).wait()

    sent = [send(part_ref, parts.at[s], s1.at[d], r1.at[s], peer)
            for d, peer in enumerate(strip_peers)]
    parts[s] = part_ref[...]
    for d in range(1, S):
        other = (s + d) % S
        arrived(parts.at[other], r1.at[other])
    coeffs = parts[0]
    for i in range(1, S):
        coeffs = coeffs + parts[i]
    coeffs_ref[...] = coeffs
    gram = lax.dot_general(coeffs, coeffs, (((0,), (0,)), ((), ())), precision=HIGHEST,
                           preferred_element_type=jnp.float32)
    local[...] = gram.reshape(NB, rows, K)

    for d, peer in enumerate(y_peers):
        block = 2 * s + ((y + d + 1) % Y) // 2
        sent.append(send(local.at[block], ybuf.at[y], s2.at[d], r2.at[y], peer))
    mine = 2 * s + y // 2
    ybuf[y] = local[mine]
    for d in range(1, Y):
        other = (y + d) % Y
        arrived(ybuf.at[other], r2.at[other])
    zbuf[z] = (ybuf[0] + ybuf[1]) + (ybuf[2] + ybuf[3])

    for d, peer in enumerate(z_peers):
        sent.append(send(zbuf.at[z], zbuf.at[z], s3.at[d], r3.at[z], peer))
    for d in range(1, Z):
        other = (z + d) % Z
        arrived(zbuf.at[other], r3.at[other])
    total = zbuf[0]
    for i in range(1, Z):
        total = total + zbuf[i]
    full[mine] = total

    fourth = strip_peers + [(f_cross, (s + d) % S) for d in range(S)]
    for d, peer in enumerate(fourth):
        sent.append(send(full.at[mine], full.at[mine], s4.at[d], r4.at[mine], peer))
    for d in range(1, NB):
        other = (mine + d) % NB
        arrived(full.at[other], r4.at[other])
    gram_ref[...] = full[...].reshape(K, K)
    for copy in sent:
        copy.wait_send()


def reduced(part, Z, S):
    frames = part.shape[0]
    rows = K // (2 * S)
    dma = pltpu.SemaphoreType.DMA
    vmem = pl.BlockSpec(memory_space=pltpu.VMEM)
    return pl.pallas_call(
        functools.partial(reduce_kernel, Z, S),
        out_shape=(jax.ShapeDtypeStruct((frames, K), jnp.float32),
                   jax.ShapeDtypeStruct((K, K), jnp.float32)),
        in_specs=[vmem],
        out_specs=(vmem, vmem),
        scratch_shapes=[
            pltpu.VMEM((S, frames, K), jnp.float32),
            pltpu.VMEM((2 * S, rows, K), jnp.float32),
            pltpu.VMEM((Y, rows, K), jnp.float32),
            pltpu.VMEM((Z, rows, K), jnp.float32),
            pltpu.VMEM((2 * S, rows, K), jnp.float32),
            dma((S,)), dma((S,)), dma((Y,)), dma((Y,)),
            dma((Z,)), dma((Z,)), dma((2 * S,)), dma((2 * S,)),
        ],
        compiler_params=pltpu.CompilerParams(collective_id=0, has_side_effects=True),
    )(part)


def pieces(x):
    high = x.astype(jnp.bfloat16).astype(jnp.float32)
    rest = x - high
    middle = rest.astype(jnp.bfloat16).astype(jnp.float32)
    return high, middle, rest - middle


def rotate_kernel(total_frames, gram_ref, prior_ref, start_ref, coeffs_ref, basis_ref,
                  basis_out, coeffs_out, sigma_out, G, RT, M):
    b = 8
    row = lax.broadcasted_iota(jnp.int32, (K, K), 0)
    column = lax.broadcasted_iota(jnp.int32, (K, K), 1)
    prior = prior_ref[...]
    G[...] = jnp.where(row == column, prior * prior, 0.0) + gram_ref[...] * (1.0 / total_frames)
    RT[...] = start_ref[...].T
    sub = lax.broadcasted_iota(jnp.int32, (b, K), 0)

    def step(_, carry):
        product_t = jnp.dot(RT[...], G[...], precision=HIGHEST,
                            preferred_element_type=jnp.float32)
        M[:, :K] = lax.dot_general(product_t, product_t, (((1,), (1,)), ((), ())),
                                   precision=HIGHEST, preferred_element_type=jnp.float32)
        M[:, K:] = product_t
        for j in range(K // b):
            at = j * b
            left, right = M[at:at + b, :K], M[at:at + b, K:]
            cols = [jnp.broadcast_to(left[:, at + i:at + i + 1], (b, K)) for i in range(b)]
            scale = jnp.zeros((b, K), jnp.float32)
            for i in range(b):
                pivot = jnp.broadcast_to(cols[i][i:i + 1], (b, K))
                scale = jnp.where(sub == i, lax.rsqrt(pivot), scale)
                if i < b - 1:
                    factor = jnp.where(sub > i, cols[i] / pivot, 0.0)
                    for c in range(i + 1, b):
                        cols[c] = cols[c] - factor * cols[c][i:i + 1]
                    left = left - factor * left[i:i + 1]
                    right = right - factor * right[i:i + 1]
            left, right = left * scale, right * scale
            RT[at:at + b, :] = right
            if at + b < K:
                h, m, l = pieces(left)
                hr, mr, lr = pieces(right)
                lhs = jnp.concatenate([h, h, m, m, h, l], axis=0).astype(jnp.bfloat16)
                rhs_l = jnp.concatenate([h, m, h, m, l, h], axis=0)
                rhs_r = jnp.concatenate([hr, mr, hr, mr, lr, hr], axis=0)
                rhs = jnp.concatenate([rhs_l, rhs_r], axis=1).astype(jnp.bfloat16)
                update = lax.dot_general(lhs, rhs, (((0,), (0,)), ((), ())),
                                         preferred_element_type=jnp.float32)
                M[at + b:, :] = M[at + b:, :] - update[at + b:, :]
        return carry

    lax.fori_loop(0, ITERS, step, 0)
    rotation_t = RT[...]
    across = (((1,), (1,)), ((), ()))
    coeffs_out[...] = lax.dot_general(coeffs_ref[...], rotation_t, across, precision=HIGHEST,
                                      preferred_element_type=jnp.float32)
    basis = basis_ref[...]
    high, middle, low = (p.astype(jnp.bfloat16) for p in pieces(rotation_t))
    basis_out[...] = (
        lax.dot_general(basis, high, across, preferred_element_type=jnp.float32)
        + (lax.dot_general(basis, middle, across, preferred_element_type=jnp.float32)
           + lax.dot_general(basis, low, across, preferred_element_type=jnp.float32))
    ).astype(jnp.bfloat16)
    curved_t = jnp.dot(rotation_t, G[...], precision=HIGHEST, preferred_element_type=jnp.float32)
    squares = lax.dot_general(jnp.ones((8, K), jnp.float32), rotation_t * curved_t, across,
                              precision=HIGHEST, preferred_element_type=jnp.float32)
    sigma_out[...] = jnp.sqrt(squares[0:1])


def rotated(gram, prior, start, coeffs, basis, total_frames):
    vmem = pl.BlockSpec(memory_space=pltpu.VMEM)
    return pl.pallas_call(
        functools.partial(rotate_kernel, total_frames),
        out_shape=(jax.ShapeDtypeStruct(basis.shape, jnp.bfloat16),
                   jax.ShapeDtypeStruct(coeffs.shape, jnp.float32),
                   jax.ShapeDtypeStruct((1, K), jnp.float32)),
        in_specs=[vmem] * 5,
        out_specs=(vmem,) * 3,
        scratch_shapes=[pltpu.VMEM((K, K), jnp.float32), pltpu.VMEM((K, K), jnp.float32),
                        pltpu.VMEM((K, 2 * K), jnp.float32)],
    )(gram, prior.reshape(1, K), start, coeffs, basis)


def body(raw_frames, dark_frame, dead_mask, frame_group, prior_sigma, start_rotation, basis):
    frame_count, strip_rows, columns = raw_frames.shape
    corrected = (
        (raw_frames.astype(jnp.float32) - dark_frame) * (1 - dead_mask).astype(jnp.float32)
    ).astype(jnp.bfloat16)
    position = jnp.arange(columns)
    offsets = position[None, :] - position[:, None]
    banded = jnp.zeros((columns, columns), jnp.float32)
    for shift_by in range(-3, 4):
        banded = banded + jnp.where(offsets == shift_by, BLUR_TAPS[shift_by + 3], 0.0)
    banded = banded.astype(jnp.bfloat16)
    column_blur = jnp.dot(
        corrected.reshape(frame_count * strip_rows, columns),
        banded,
        preferred_element_type=jnp.float32,
    )
    column_blur = column_blur.reshape(frame_count, strip_rows, columns)
    padded = extended(column_blur, (("strips", 1),), 3)
    row_blur = BLUR_TAPS[0] * padded[:, 0:strip_rows, :]
    for offset in range(1, 7):
        row_blur = row_blur + BLUR_TAPS[offset] * padded[:, offset : offset + strip_rows, :]
    frame_weight = jnp.power(
        jnp.float32(DECAY_RATE), (GROUPS - 1 - frame_group).astype(jnp.float32)
    )
    weighted = (
        (frame_weight[:, None, None] * row_blur)
        .astype(jnp.bfloat16)
        .reshape(frame_count, strip_rows * columns)
    )
    partial_value = jnp.dot(
        weighted,
        lax.all_gather(basis, "frames", axis=0, tiled=True),
        preferred_element_type=jnp.float32,
    )
    frames, strips = lax.axis_size("frames"), lax.axis_size("strips")
    coeffs, summed_gram = reduced(partial_value, frames // Y, strips)
    new_basis, new_coeffs, new_sigma = rotated(
        summed_gram, prior_sigma, start_rotation, coeffs, basis, frame_count * frames)
    return (new_basis, new_coeffs, new_sigma.reshape(K))


def solution(mesh):
    placed = (
        P("frames", "strips", None),
        P("strips", None),
        P("strips", None),
        P("frames"),
        P(),
        P(),
        P(("strips", "frames"), None),
    )
    return jax.shard_map(
        body,
        mesh=mesh,
        in_specs=placed,
        out_specs=(P(("strips", "frames"), None), P("frames", None), P()),
        check_vma=False,
    )
```

```python
import functools

import jax
import jax.numpy as jnp
from jax import lax
from jax.experimental import pallas as pl
from jax.experimental.pallas import tpu as pltpu
from jax.sharding import PartitionSpec as P

GROUPS = 8
ITERS = 4
K = 128
Y = 4
SPLIT = 192

BLUR_TAPS = (1.0 / 64, 6.0 / 64, 15.0 / 64, 20.0 / 64, 15.0 / 64, 6.0 / 64, 1.0 / 64)
DECAY_RATE = 0.7
MESH = pl.DeviceIdType.MESH
HIGHEST = lax.Precision.HIGHEST


def window_kernel(Z, S, corrected_ref, weight_ref, basis_ref, coeffs_ref, gram_ref,
                  full_basis, halo, blurred, weighted, part,
                  parts, local, ybuf, zbuf, full,
                  own_sem, halo_send, halo_recv, ay_send, az_send, bz_send, by_send,
                  a_recv, a_recv2, b_recv, b_recv2, bz_recv2,
                  s1, r1, s2, r2, s3, r3, s4, r4):
    f, s = lax.axis_index("frames"), lax.axis_index("strips")
    z, y = f // Y, f % Y
    R, D, W = corrected_ref.shape
    NB = 2 * S
    rows = K // NB
    f_cross = z * Y + (y + 2) % Y
    strip_peers = [(f, (s + d) % S) for d in range(1, S)]
    y_peers = [(z * Y + (y + d) % Y, s) for d in range(1, Y)]
    z_peers = [(((z + d) % Z) * Y + y, s) for d in range(1, Z)]
    cross_peers = [(f_cross, (s + d) % S) for d in range(1, S)]
    everyone = strip_peers + y_peers + z_peers + cross_peers
    z_up, z_down, y_up, y_down = z_peers[0], z_peers[-1], y_peers[0], y_peers[-1]
    strip_up, strip_down = strip_peers[0], strip_peers[-1]

    barrier = pltpu.get_barrier_semaphore()
    for peer in everyone:
        pl.semaphore_signal(barrier, inc=1, device_id=peer, device_id_type=MESH)
    own = pltpu.make_async_copy(basis_ref, full_basis.at[f], own_sem)
    own.start()

    offset = (lax.broadcasted_iota(jnp.int32, (W, W), 1)
              - lax.broadcasted_iota(jnp.int32, (W, W), 0))
    banded = jnp.zeros((W, W), jnp.float32)
    for e in range(-3, 4):
        banded = jnp.where(offset == e, BLUR_TAPS[e + 3], banded)
    banded = banded.astype(jnp.bfloat16)
    weight = jnp.broadcast_to(weight_ref[...], (D, W))

    def column_blur(start, count):
        def one(i, carry):
            r = start + i
            blurred[r + 3] = jnp.dot(corrected_ref[r], banded,
                                     preferred_element_type=jnp.float32)
            return carry
        lax.fori_loop(0, count, one, 0)

    def halo_blur():
        for side in range(2):
            arrived(halo.at[side], halo_recv.at[side])
            inside = s > 0 if side == 0 else s < S - 1
            for i in range(3):
                value = jnp.dot(halo[side, i], banded, preferred_element_type=jnp.float32)
                blurred[i if side == 0 else R + 3 + i] = jnp.where(inside, value, 0.0)

    def row_blur(start, count):
        def one(i, carry):
            r = start + i
            value = BLUR_TAPS[0] * blurred[r]
            for e in range(1, 7):
                value = value + BLUR_TAPS[e] * blurred[r + e]
            weighted[r] = (weight * value).astype(jnp.bfloat16)
            return carry
        lax.fori_loop(0, count, one, 0)

    def send(src, dst, ssem, rsem, peer):
        copy = pltpu.make_async_remote_copy(
            src_ref=src, dst_ref=dst, send_sem=ssem, recv_sem=rsem,
            device_id=peer, device_id_type=MESH)
        copy.start()
        return copy

    def arrived(ref, sem):
        pltpu.make_async_copy(ref, ref, sem).wait()

    column_blur(0, R // 4)
    tasks = [functools.partial(column_blur, q * (R // 4), R // 4) for q in range(1, 4)]
    tasks.append(halo_blur)
    tasks += [functools.partial(row_blur, q * (R // 4), R // 4) for q in range(4)]
    own.wait()
    pl.semaphore_wait(barrier, len(everyone))

    cut = SPLIT
    rest = W - cut
    half = Z // 2

    def a(slot, lo=0, hi=cut):
        return full_basis.at[slot, pl.ds(lo, hi - lo)]

    def b(slot, lo=0, hi=rest):
        return full_basis.at[slot, pl.ds(cut + lo, hi - lo)]

    def pass_on(ref, ssem, rsem, peer):
        send(ref, ref, ssem.at[0], rsem, peer)

    pass_on(b(f), bz_send, b_recv.at[f], z_up)
    pass_on(b(f), bz_send, b_recv.at[f], z_down)
    for peer in y_peers:
        pass_on(a(f), ay_send, a_recv.at[f], peer)
    pass_on(a(f), az_send, a_recv.at[f], z_up)
    pass_on(a(f), az_send, a_recv.at[f], z_down)
    pass_on(b(f), by_send, b_recv.at[f], y_up)
    pass_on(b(f), by_send, b_recv.at[f], y_down)
    sent = [send(corrected_ref.at[pl.ds(R - 3, 3)], halo.at[0], halo_send.at[0],
                 halo_recv.at[0], strip_up),
            send(corrected_ref.at[pl.ds(0, 3)], halo.at[1], halo_send.at[1],
                 halo_recv.at[1], strip_down)]
    for d in range(1, Y):
        slot = z * Y + (y + d) % Y
        arrived(a(slot), a_recv.at[slot])
        pass_on(a(slot), az_send, a_recv.at[slot], z_up)
        pass_on(a(slot), az_send, a_recv.at[slot], z_down)

    def across_y(zz):
        below, above = zz * Y + (y + Y - 1) % Y, zz * Y + (y + 1) % Y
        arrived(b(below), b_recv.at[below])
        pass_on(b(below, 0, rest // 2), by_send, b_recv.at[below], y_up)
        arrived(b(above), b_recv.at[above])
        pass_on(b(above, rest // 2, rest), by_send, b_recv2.at[zz], y_down)

    for k in range(1, half):
        lower, upper = (z + Z - k) % Z, (z + k) % Z
        last = k == half - 1
        for zz, peer, side in ((lower, z_up, 0), (upper, z_down, 1)):
            slot = zz * Y + y
            arrived(b(slot), b_recv.at[slot])
            if not last:
                pass_on(b(slot), bz_send, b_recv.at[slot], peer)
            elif side == 0:
                pass_on(b(slot, 0, rest // 2), bz_send, b_recv.at[slot], peer)
            else:
                pass_on(b(slot, rest // 2, rest), bz_send, bz_recv2.at[0], peer)
            pass_on(b(slot), by_send, b_recv.at[slot], y_up)
            pass_on(b(slot), by_send, b_recv.at[slot], y_down)
        for c in range(Y):
            for zz, peer, side in ((lower, z_up, 0), (upper, z_down, 1)):
                slot = zz * Y + c
                arrived(a(slot), a_recv.at[slot])
                if not last:
                    pass_on(a(slot), az_send, a_recv.at[slot], peer)
                elif side == 0:
                    pass_on(a(slot, 0, cut // 2), az_send, a_recv.at[slot], peer)
                else:
                    pass_on(a(slot, cut // 2, cut), az_send, a_recv2.at[c], peer)
        if k == 1:
            across_y(z)
        else:
            across_y((z + Z - k + 1) % Z)
            across_y((z + k - 1) % Z)
        share = -(-len(tasks) // (half - k + 1))
        for task in tasks[:share]:
            task()
        tasks = tasks[share:]
    far = (z + half) % Z
    slot = far * Y + y
    arrived(b(slot, 0, rest // 2), b_recv.at[slot])
    arrived(b(slot, rest // 2, rest), bz_recv2.at[0])
    pass_on(b(slot), by_send, b_recv.at[slot], y_up)
    pass_on(b(slot), by_send, b_recv.at[slot], y_down)
    across_y((z + Z - half + 1) % Z)
    if half > 2:
        across_y((z + half - 1) % Z)
    else:
        across_y((z + 1) % Z)
    for task in tasks:
        task()
    for c in range(Y):
        slot = far * Y + c
        arrived(a(slot, 0, cut // 2), a_recv.at[slot])
        arrived(a(slot, cut // 2, cut), a_recv2.at[c])
    across_y(far)
    for d in range(Z):
        zz = (z + d) % Z
        slot = zz * Y + (y + 2) % Y
        arrived(b(slot, 0, rest // 2), b_recv.at[slot])
        arrived(b(slot, rest // 2, rest), b_recv2.at[zz])

    def project(i, total):
        for r in range(4):
            total = total + jnp.dot(weighted[4 * i + r], full_basis[4 * i + r],
                                    preferred_element_type=jnp.float32)
        return total

    part[...] = lax.fori_loop(0, R // 4, project, jnp.zeros((D, K), jnp.float32))

    sent += [send(part, parts.at[s], s1.at[d], r1.at[s], peer)
             for d, peer in enumerate(strip_peers)]
    parts[s] = part[...]
    for d in range(1, S):
        other = (s + d) % S
        arrived(parts.at[other], r1.at[other])
    coeffs = parts[0]
    for i in range(1, S):
        coeffs = coeffs + parts[i]
    coeffs_ref[...] = coeffs
    gram = lax.dot_general(coeffs, coeffs, (((0,), (0,)), ((), ())), precision=HIGHEST,
                           preferred_element_type=jnp.float32)
    local[...] = gram.reshape(NB, rows, K)

    for d, peer in enumerate(y_peers):
        block = 2 * s + ((y + d + 1) % Y) // 2
        sent.append(send(local.at[block], ybuf.at[y], s2.at[d], r2.at[y], peer))
    mine = 2 * s + y // 2
    ybuf[y] = local[mine]
    for d in range(1, Y):
        other = (y + d) % Y
        arrived(ybuf.at[other], r2.at[other])
    zbuf[z] = (ybuf[0] + ybuf[1]) + (ybuf[2] + ybuf[3])

    for d, peer in enumerate(z_peers):
        sent.append(send(zbuf.at[z], zbuf.at[z], s3.at[d], r3.at[z], peer))
    for d in range(1, Z):
        other = (z + d) % Z
        arrived(zbuf.at[other], r3.at[other])
    total = zbuf[0]
    for i in range(1, Z):
        total = total + zbuf[i]
    full[mine] = total

    fourth = strip_peers + [(f_cross, (s + d) % S) for d in range(S)]
    for d, peer in enumerate(fourth):
        sent.append(send(full.at[mine], full.at[mine], s4.at[d], r4.at[mine], peer))
    for d in range(1, NB):
        other = (mine + d) % NB
        arrived(full.at[other], r4.at[other])
    gram_ref[...] = full[...].reshape(K, K)

    for copy in sent:
        copy.wait_send()
    arrived(full_basis.at[pl.ds(0, Y - 1), pl.ds(0, cut)], ay_send.at[0])
    arrived(full_basis.at[pl.ds(0, Y * (Z - 1)), pl.ds(0, cut)], az_send.at[0])
    arrived(full_basis.at[pl.ds(0, Z - 1), pl.ds(cut, rest)], bz_send.at[0])
    arrived(full_basis.at[pl.ds(0, 3 * Z), pl.ds(cut, rest)], by_send.at[0])


def windowed(corrected, weight, basis, Z, S):
    R, D, W = corrected.shape
    rows = K // (2 * S)
    dma = pltpu.SemaphoreType.DMA
    vmem = pl.BlockSpec(memory_space=pltpu.VMEM)
    f32, bf16 = jnp.float32, jnp.bfloat16
    return pl.pallas_call(
        functools.partial(window_kernel, Z, S),
        out_shape=(jax.ShapeDtypeStruct((D, K), f32), jax.ShapeDtypeStruct((K, K), f32)),
        in_specs=[vmem] * 3,
        out_specs=(vmem, vmem),
        scratch_shapes=[
            pltpu.VMEM((Z * Y, W, K), bf16),
            pltpu.VMEM((2, 3, D, W), bf16),
            pltpu.VMEM((R + 6, D, W), f32),
            pltpu.VMEM((R, D, W), bf16),
            pltpu.VMEM((D, K), f32),
            pltpu.VMEM((S, D, K), f32),
            pltpu.VMEM((2 * S, rows, K), f32),
            pltpu.VMEM((Y, rows, K), f32),
            pltpu.VMEM((Z, rows, K), f32),
            pltpu.VMEM((2 * S, rows, K), f32),
            dma, dma((2,)), dma((2,)), dma((1,)), dma((1,)), dma((1,)), dma((1,)),
            dma((Z * Y,)), dma((Y,)), dma((Z * Y,)), dma((Z,)), dma((1,)),
            dma((S,)), dma((S,)), dma((Y,)), dma((Y,)),
            dma((Z,)), dma((Z,)), dma((2 * S,)), dma((2 * S,)),
        ],
        compiler_params=pltpu.CompilerParams(collective_id=0, has_side_effects=True),
    )(corrected, weight, basis)


def pieces(x):
    high = x.astype(jnp.bfloat16).astype(jnp.float32)
    rest = x - high
    middle = rest.astype(jnp.bfloat16).astype(jnp.float32)
    return high, middle, rest - middle


def rotate_kernel(total_frames, gram_ref, prior_ref, start_ref, coeffs_ref, basis_ref,
                  basis_out, coeffs_out, sigma_out, G, RT, M):
    b = 8
    row = lax.broadcasted_iota(jnp.int32, (K, K), 0)
    column = lax.broadcasted_iota(jnp.int32, (K, K), 1)
    prior = prior_ref[...]
    G[...] = jnp.where(row == column, prior * prior, 0.0) + gram_ref[...] * (1.0 / total_frames)
    RT[...] = start_ref[...].T
    sub = lax.broadcasted_iota(jnp.int32, (b, K), 0)

    def step(_, carry):
        product_t = jnp.dot(RT[...], G[...], precision=HIGHEST,
                            preferred_element_type=jnp.float32)
        M[:, :K] = lax.dot_general(product_t, product_t, (((1,), (1,)), ((), ())),
                                   precision=HIGHEST, preferred_element_type=jnp.float32)
        M[:, K:] = product_t
        for j in range(K // b):
            at = j * b
            left, right = M[at:at + b, :K], M[at:at + b, K:]
            cols = [jnp.broadcast_to(left[:, at + i:at + i + 1], (b, K)) for i in range(b)]
            scale = jnp.zeros((b, K), jnp.float32)
            for i in range(b):
                pivot = jnp.broadcast_to(cols[i][i:i + 1], (b, K))
                scale = jnp.where(sub == i, lax.rsqrt(pivot), scale)
                if i < b - 1:
                    factor = jnp.where(sub > i, cols[i] / pivot, 0.0)
                    for c in range(i + 1, b):
                        cols[c] = cols[c] - factor * cols[c][i:i + 1]
                    left = left - factor * left[i:i + 1]
                    right = right - factor * right[i:i + 1]
            left, right = left * scale, right * scale
            RT[at:at + b, :] = right
            if at + b < K:
                h, m, l = pieces(left)
                hr, mr, lr = pieces(right)
                lhs = jnp.concatenate([h, h, m, m, h, l], axis=0).astype(jnp.bfloat16)
                rhs_l = jnp.concatenate([h, m, h, m, l, h], axis=0)
                rhs_r = jnp.concatenate([hr, mr, hr, mr, lr, hr], axis=0)
                rhs = jnp.concatenate([rhs_l, rhs_r], axis=1).astype(jnp.bfloat16)
                update = lax.dot_general(lhs, rhs, (((0,), (0,)), ((), ())),
                                         preferred_element_type=jnp.float32)
                M[at + b:, :] = M[at + b:, :] - update[at + b:, :]
        return carry

    lax.fori_loop(0, ITERS, step, 0)
    rotation_t = RT[...]
    across = (((1,), (1,)), ((), ()))
    coeffs_out[...] = lax.dot_general(coeffs_ref[...], rotation_t, across, precision=HIGHEST,
                                      preferred_element_type=jnp.float32)
    basis = basis_ref[...]
    high, middle, low = (p.astype(jnp.bfloat16) for p in pieces(rotation_t))
    basis_out[...] = (
        lax.dot_general(basis, high, across, preferred_element_type=jnp.float32)
        + (lax.dot_general(basis, middle, across, preferred_element_type=jnp.float32)
           + lax.dot_general(basis, low, across, preferred_element_type=jnp.float32))
    ).astype(jnp.bfloat16)
    curved_t = jnp.dot(rotation_t, G[...], precision=HIGHEST, preferred_element_type=jnp.float32)
    squares = lax.dot_general(jnp.ones((8, K), jnp.float32), rotation_t * curved_t, across,
                              precision=HIGHEST, preferred_element_type=jnp.float32)
    sigma_out[...] = jnp.sqrt(squares[0:1])


def rotated(gram, prior, start, coeffs, basis, total_frames):
    vmem = pl.BlockSpec(memory_space=pltpu.VMEM)
    return pl.pallas_call(
        functools.partial(rotate_kernel, total_frames),
        out_shape=(jax.ShapeDtypeStruct(basis.shape, jnp.bfloat16),
                   jax.ShapeDtypeStruct(coeffs.shape, jnp.float32),
                   jax.ShapeDtypeStruct((1, K), jnp.float32)),
        in_specs=[vmem] * 5,
        out_specs=(vmem,) * 3,
        scratch_shapes=[pltpu.VMEM((K, K), jnp.float32), pltpu.VMEM((K, K), jnp.float32),
                        pltpu.VMEM((K, 2 * K), jnp.float32)],
    )(gram, prior.reshape(1, K), start, coeffs, basis)


def body(raw_frames, dark_frame, dead_mask, frame_group, prior_sigma, start_rotation, basis):
    frame_count, strip_rows, columns = raw_frames.shape
    corrected = (
        (raw_frames.astype(jnp.float32) - dark_frame) * (1 - dead_mask).astype(jnp.float32)
    ).astype(jnp.bfloat16)
    frame_weight = jnp.power(
        jnp.float32(DECAY_RATE), (GROUPS - 1 - frame_group).astype(jnp.float32)
    )
    frames, strips = lax.axis_size("frames"), lax.axis_size("strips")
    coeffs, summed_gram = windowed(
        corrected.transpose(1, 0, 2), frame_weight[:, None], basis, frames // Y, strips)
    new_basis, new_coeffs, new_sigma = rotated(
        summed_gram, prior_sigma, start_rotation, coeffs, basis, frame_count * frames)
    return (new_basis, new_coeffs, new_sigma.reshape(K))


def solution(mesh):
    placed = (
        P("frames", "strips", None),
        P("strips", None),
        P("strips", None),
        P("frames"),
        P(),
        P(),
        P(("strips", "frames"), None),
    )
    return jax.shard_map(
        body,
        mesh=mesh,
        in_specs=placed,
        out_specs=(P(("strips", "frames"), None), P("frames", None), P()),
        check_vma=False,
    )
```
